32 devices in a mesh: ctx: 8 (over z, y), fsdp: 4 (over x, core).
Axes of the slice: x: 2, y: 2, z: 4, core: 2. Of those that a mesh axis runs over, the one named last changes fastest.
Arguments:
- tokens: bfloat16 [4096, 768], P(('ctx', 'fsdp')), may hold values from -8 to 8
- cotangent: bfloat16 [4096, 768], P(('ctx', 'fsdp')), may hold values from -6 to 6
- pair_order: int32 [4, 8], P('fsdp'), may hold values from 0 to 7, each once within a row
- gain_attn: bfloat16 [768], P('fsdp'), may hold values from 0.5 to 1.5
- shift_attn: bfloat16 [768], P('fsdp'), may hold values from -1.5 to 1.5
- gain_mlp: bfloat16 [768], P('fsdp'), may hold values from 0.5 to 1.5
- shift_mlp: bfloat16 [768], P('fsdp'), may hold values from -1.5 to 1.5
- qkv_weight: bfloat16 [768, 2304], P('fsdp'), may hold values from -1.5 to 1.5
- qkv_bias: bfloat16 [2304], P('fsdp'), may hold values from -0.099609375 to 0.099609375
- dense_weight: bfloat16 [768, 768], P('fsdp'), may hold values from -3.5 to 3.5
- up_weight: bfloat16 [768, 3072], P('fsdp'), may hold values from -0.21875 to 0.21875
- up_bias: bfloat16 [3072], P('fsdp'), may hold values from -1.5 to 1.5
- down_weight: bfloat16 [3072, 768], P('fsdp'), may hold values from -0.109375 to 0.109375
- out_bias: bfloat16 [768], P('fsdp'), may hold values from -1.5 to 1.5
Outputs:
- layer_out: bfloat16 [4096, 768], P(('ctx', 'fsdp'))
- input_grad: float32 [4096, 768], P(('ctx', 'fsdp'))
- attngain_grad: float32 [768], P('fsdp')
- attnshift_grad: float32 [768], P('fsdp')
- mlpgain_grad: float32 [768], P('fsdp')
- mlpshift_grad: float32 [768], P('fsdp')
- qkvweight_grad: float32 [768, 2304], P('fsdp')
- qkvbias_grad: float32 [2304], P('fsdp')
- dense_grad: float32 [768, 768], P('fsdp')
- upweight_grad: float32 [768, 3072], P('fsdp')
- upbias_grad: float32 [3072], P('fsdp')
- downweight_grad: float32 [3072, 768], P('fsdp')
- outbias_grad: float32 [768], P('fsdp')
The draws below stay inside these ranges and needn't reach their ends.
Inputs may be any that keep to these rules, and one draw needn't show every extreme that they name: Each row of pair_order holds every number 0 to 7 once; index c of ctx holds blocks pair_order[f, c] and 15 - pair_order[f, c] of sequence f.
All inputs are finite; a program needn't handle non-finite values.
Results may differ from the reference program's by a relative error of at most 0.009.
Values may be sent and summed in bfloat16 or wider, within the bound.
No kernel may reach another device: no remote copies, remote signals or barrier semaphores. Data moves between devices by JAX's collectives and lax.ppermute only.
A program may use at most 192 MiB of HBM per device.

```python
import math
import jax
import jax.numpy as jnp
from jax import lax

D = 768
HEADS = 12
HEAD_DIM = 64
ROT = 16
FF = 3072
TOK_DEV = 128
LENGTH = 1024
SEQS = 4
TOKENS = 4096
N_CTX = 8
N_FSDP = 4


def draw_tokens(key, part):
    row_key, column_key, noise_key = jax.random.split(key, 3)
    row_scale = jnp.exp(jax.random.uniform(row_key, (TOKENS, 1), jnp.float32, math.log(0.3), math.log(3.0)))
    column_scale = jnp.exp(jax.random.uniform(column_key, (1, D), jnp.float32, math.log(0.3), math.log(3.0)))
    noise = jnp.clip(jax.random.normal(noise_key, (TOKENS, D), jnp.float32), -3.0, 3.0)
    return jnp.clip(noise * row_scale * column_scale, -8.0, 8.0).astype(jnp.bfloat16)


def draw_qkv_weight(key, part):
    base = jnp.clip(jax.random.normal(key, (D, 3 * D), jnp.float32), -4.0, 4.0)
    base = base / math.sqrt(D)
    return jnp.clip(base, -1.5, 1.5).astype(jnp.bfloat16)


def shard_levels(own_key, dims, shards, low, high):
    factor_of, own = 1.0, jax.random.fold_in(own_key, 6)
    for dim, blocks in shards:
        draws = jnp.exp(jax.random.uniform(jax.random.fold_in(own, dim), (blocks,), jnp.float32, low / len(shards), high / len(shards)))
        factor_of = factor_of * jnp.repeat(draws, dims[dim] // blocks).reshape([-1 if axis == dim else 1 for axis in range(len(dims))])
    return factor_of


def scatter_about(key, extent, spread, most, shards=(), kind=jnp.bfloat16):
    level = shard_levels(key, extent, shards, -0.22, 0.18) if shards else 1.0
    entries = jax.random.normal(key, extent, jnp.float32) * spread * level
    return jnp.minimum(jnp.maximum(entries, -most), most).astype(kind)


def setup_inputs(seed: int = 0) -> dict:
    splits = jax.random.split(jax.random.key(seed), 15)
    return {
        "tokens": draw_tokens(jax.random.fold_in(splits[14], 71), 0),
        "cotangent": scatter_about(splits[1], (TOKENS, D), 1.0, 6.0, ((0, 32),)),
        "pair_order": jax.vmap(lambda own: jax.random.permutation(own, N_CTX))(jax.random.split(splits[2], SEQS)).reshape((SEQS, N_CTX)).astype(jnp.int32),
        "gain_attn": jnp.clip(1.0 + 0.1 * jax.random.normal(splits[3], (D,), jnp.float32), 0.5, 1.5).astype(jnp.bfloat16),
        "shift_attn": scatter_about(splits[4], (D,), 0.3, 1.5, ((0, 4),)),
        "gain_mlp": jnp.clip(1.0 + 0.1 * jax.random.normal(splits[5], (D,), jnp.float32), 0.5, 1.5).astype(jnp.bfloat16),
        "shift_mlp": scatter_about(splits[6], (D,), 0.3, 1.5, ((0, 4),)),
        "qkv_weight": draw_qkv_weight(jax.random.fold_in(splits[14], 71), 0),
        "qkv_bias": scatter_about(splits[8], (3 * D,), 0.02, 0.099609375, ((0, 4),)),
        "dense_weight": scatter_about(splits[9], (D, D), (max(1, D * 4 // LENGTH)) ** -0.5, 3.5, ((0, 4),)),
        "up_weight": scatter_about(splits[10], (D, FF), D ** -0.5, 0.21875, ((0, 4),)),
        "up_bias": scatter_about(splits[11], (FF,), 0.3, 1.5, ((0, 4),)),
        "down_weight": scatter_about(splits[12], (FF, D), FF ** -0.5, 0.109375, ((0, 4),)),
        "out_bias": scatter_about(splits[13], (D,), 0.3, 1.5, ((0, 4),)),
    }


EPSILON = 1e-05

def normalize(values, gain, shift):
    row_mean = lax.optimization_barrier(jnp.mean(values, axis=-1, keepdims=True))
    centred = values - row_mean
    variance = lax.optimization_barrier(jnp.mean(centred * centred, axis=-1, keepdims=True))
    inverse = lax.rsqrt(variance + EPSILON)
    normed = centred * inverse
    return (normed * gain.astype(jnp.float32) + shift.astype(jnp.float32), normed, inverse)

def normalize_back(upstream, normed, inverse, gain):
    scaled = upstream * gain.astype(jnp.float32)
    first_mean = lax.optimization_barrier(jnp.mean(scaled, axis=-1, keepdims=True))
    second_mean = lax.optimization_barrier(jnp.mean(scaled * normed, axis=-1, keepdims=True))
    into_grad = inverse * (scaled - first_mean - normed * second_mean)
    return (into_grad, lax.optimization_barrier(jnp.sum(upstream * normed, axis=0)), lax.optimization_barrier(jnp.sum(upstream, axis=0)))

def block_positions(first_block, count_rows, count_ctx):
    half_rows = count_rows // 2
    offsets = jnp.arange(count_rows, dtype=jnp.int32)
    early_pos = first_block * half_rows + offsets
    late_pos = (2 * count_ctx - 1 - first_block) * half_rows + offsets - half_rows
    return jnp.where(offsets < half_rows, early_pos, late_pos).astype(jnp.int32)

def rotary_tables(positions):
    half_rot = ROT // 2
    frequency = jnp.power(10000.0, -2.0 * jnp.arange(half_rot, dtype=jnp.float32) / ROT)
    angles = positions.astype(jnp.float32)[:, None] * frequency[None, :]
    return (jnp.cos(angles), jnp.sin(angles))

def rotate(values, cosine, sine_table):
    half_rot = ROT // 2
    first_half = values[..., :half_rot]
    second = values[..., half_rot:ROT]
    cos_wide = cosine[:, None, :]
    sin_wide = sine_table[:, None, :]
    return jnp.concatenate([first_half * cos_wide - second * sin_wide, second * cos_wide + first_half * sin_wide, values[..., ROT:]], axis=-1)

def gelu_parts(values):
    cumulative = 0.5 * (1.0 + lax.erf(values * 0.7071067811865476))
    density = jnp.exp(-0.5 * values * values) * 0.3989422804014327
    return (values * cumulative, cumulative + values * density)

def attend(queries, key_heads, value_heads, causal, score_scale):
    scores = jnp.einsum('qhd,khd->hqk', queries.astype(jnp.float32), key_heads.astype(jnp.float32)) * score_scale
    scores = jnp.where(causal[None], scores, -jnp.inf)
    row_peak = lax.optimization_barrier(jnp.max(scores, axis=-1, keepdims=True))
    weight_sum = lax.optimization_barrier(jnp.sum(jnp.exp(scores - row_peak), axis=-1, keepdims=True))
    logsum = row_peak + jnp.log(weight_sum)
    weights_half = jnp.exp(scores - logsum).astype(jnp.bfloat16)
    mixed = jnp.einsum('hqk,khd->qhd', weights_half.astype(jnp.float32), value_heads.astype(jnp.float32))
    return (mixed, logsum[..., 0])

def attend_back(queries, key_heads, value_heads, causal, logsum, attn_mix, mix_grad, score_scale):
    scores = jnp.einsum('qhd,khd->hqk', queries.astype(jnp.float32), key_heads.astype(jnp.float32)) * score_scale
    weights_full = jnp.where(causal[None], jnp.exp(scores - logsum[..., None]), 0.0)
    weights_half = weights_full.astype(jnp.bfloat16)
    grad_wide = mix_grad.astype(jnp.float32)
    value_grad = jnp.einsum('hqk,qhd->khd', weights_half.astype(jnp.float32), grad_wide)
    weight_grad = jnp.einsum('qhd,khd->hqk', grad_wide, value_heads.astype(jnp.float32))
    row_delta = lax.optimization_barrier(jnp.sum(grad_wide * attn_mix.astype(jnp.float32), axis=-1)).T
    score_grad = (weights_full * (weight_grad - row_delta[:, :, None]) * score_scale).astype(jnp.bfloat16)
    query_grad = jnp.einsum('hqk,khd->qhd', score_grad.astype(jnp.float32), key_heads.astype(jnp.float32))
    key_grad = jnp.einsum('hqk,qhd->khd', score_grad.astype(jnp.float32), queries.astype(jnp.float32))
    return (query_grad, key_grad, value_grad)

def reference(tokens, cotangent, pair_order, gain_attn, shift_attn, gain_mlp, shift_mlp, qkv_weight, qkv_bias, dense_weight, up_weight, up_bias, down_weight, out_bias):
    length = TOK_DEV * N_CTX
    width = D
    score_scale = 1.0 / math.sqrt(HEAD_DIM)
    block_rows = math.gcd(length, 512)
    count_blocks = length // block_rows

    def regroup(values):
        return values.reshape(N_CTX, N_FSDP, TOK_DEV, width).transpose(1, 0, 2, 3).reshape(N_FSDP, length, width)

    def ungroup(values):
        return values.reshape(N_FSDP, N_CTX, TOK_DEV, width).transpose(1, 0, 2, 3).reshape(N_CTX * N_FSDP * TOK_DEV, width)
    positions = block_positions(pair_order[:, :, None], TOK_DEV, N_CTX).reshape(N_FSDP, length)

    def one_sequence(totals, inputs):
        seq_tokens, seq_grad, seq_pos = inputs
        cosine, sine_table = rotary_tables(seq_pos)
        residual = seq_tokens.astype(jnp.float32)
        attn_norm, normed_attn, inverse_attn = normalize(residual, gain_attn, shift_attn)
        attn_in = attn_norm.astype(jnp.bfloat16)
        projected = jnp.dot(attn_in, qkv_weight, preferred_element_type=jnp.float32) + qkv_bias.astype(jnp.float32)
        heads_all = projected.reshape(length, 3, HEADS, HEAD_DIM)
        queries = rotate(heads_all[:, 0], cosine, sine_table).astype(jnp.bfloat16)
        key_heads = rotate(heads_all[:, 1], cosine, sine_table).astype(jnp.bfloat16)
        value_heads = heads_all[:, 2].astype(jnp.bfloat16)
        query_blocks = queries.reshape(count_blocks, block_rows, HEADS, HEAD_DIM)
        pos_blocks = seq_pos.reshape(count_blocks, block_rows)

        def forward_block(carry, blocks):
            block_query, block_pos = blocks
            causal = seq_pos[None, :] <= block_pos[:, None]
            return (carry, attend(block_query, key_heads, value_heads, causal, score_scale))
        _, (mixed, logsum) = lax.scan(forward_block, jnp.zeros((), jnp.float32), (query_blocks, pos_blocks))
        attn_mix = mixed.reshape(length, HEADS, HEAD_DIM).astype(jnp.bfloat16)
        mix_flat = attn_mix.reshape(length, width)
        mlp_norm, normed_mlp, inverse_mlp = normalize(residual, gain_mlp, shift_mlp)
        mlp_in = mlp_norm.astype(jnp.bfloat16)
        hidden_pre = jnp.dot(mlp_in, up_weight, preferred_element_type=jnp.float32) + up_bias.astype(jnp.float32)
        activated, slope = gelu_parts(hidden_pre)
        hidden = activated.astype(jnp.bfloat16)
        summed = residual + jnp.dot(mix_flat, dense_weight, preferred_element_type=jnp.float32) + jnp.dot(hidden, down_weight, preferred_element_type=jnp.float32) + out_bias.astype(jnp.float32)
        layer_out = summed.astype(jnp.bfloat16)
        grad_out = seq_grad.astype(jnp.float32)
        outbias_part = lax.optimization_barrier(jnp.sum(grad_out, axis=0))
        down_part = jnp.dot(hidden.T, seq_grad, preferred_element_type=jnp.float32)
        dense_part = jnp.dot(mix_flat.T, seq_grad, preferred_element_type=jnp.float32)
        pre_grad = jnp.dot(seq_grad, down_weight.T, preferred_element_type=jnp.float32) * slope
        upbias_part = lax.optimization_barrier(jnp.sum(pre_grad, axis=0))
        pre_half = pre_grad.astype(jnp.bfloat16)
        up_part = jnp.dot(mlp_in.T, pre_half, preferred_element_type=jnp.float32)
        mlp_in_grad = jnp.dot(pre_half, up_weight.T, preferred_element_type=jnp.float32)
        mix_grad = jnp.dot(seq_grad, dense_weight.T, preferred_element_type=jnp.float32).astype(jnp.bfloat16).reshape(length, HEADS, HEAD_DIM)

        def backward_block(carry, blocks):
            block_query, block_pos, block_logsum, block_mix, block_grad = blocks
            causal = seq_pos[None, :] <= block_pos[:, None]
            query_grad, key_grad, value_grad = attend_back(block_query, key_heads, value_heads, causal, block_logsum, block_mix, block_grad, score_scale)
            return ((carry[0] + key_grad, carry[1] + value_grad), query_grad)
        zero_heads = jnp.zeros((length, HEADS, HEAD_DIM), jnp.float32)
        block_shape = (count_blocks, block_rows, HEADS, HEAD_DIM)
        (key_grad, value_grad), query_grad = lax.scan(backward_block, (zero_heads, zero_heads), (query_blocks, pos_blocks, logsum, attn_mix.reshape(block_shape), mix_grad.reshape(block_shape)))
        query_grad = query_grad.reshape(length, HEADS, HEAD_DIM)
        proj_grad = jnp.stack([rotate(query_grad, cosine, -sine_table), rotate(key_grad, cosine, -sine_table), value_grad], axis=1).reshape(length, 3 * width)
        qkvbias_part = lax.optimization_barrier(jnp.sum(proj_grad, axis=0))
        proj_half = proj_grad.astype(jnp.bfloat16)
        qkv_part = jnp.dot(attn_in.T, proj_half, preferred_element_type=jnp.float32)
        attn_in_grad = jnp.dot(proj_half, qkv_weight.T, preferred_element_type=jnp.float32)
        into_attn, gainattn_part, shiftattn_part = normalize_back(attn_in_grad, normed_attn, inverse_attn, gain_attn)
        into_mlp, gainmlp_part, shiftmlp_part = normalize_back(mlp_in_grad, normed_mlp, inverse_mlp, gain_mlp)
        input_grad = grad_out + into_attn + into_mlp
        parts = (gainattn_part, shiftattn_part, gainmlp_part, shiftmlp_part, qkv_part, qkvbias_part, dense_part, up_part, upbias_part, down_part, outbias_part)
        totals = tuple((total + part for total, part in zip(totals, parts)))
        return (totals, (layer_out, input_grad))
    zero_totals = (jnp.zeros((D,), jnp.float32), jnp.zeros((D,), jnp.float32), jnp.zeros((D,), jnp.float32), jnp.zeros((D,), jnp.float32), jnp.zeros((D, 3 * D), jnp.float32), jnp.zeros((3 * D,), jnp.float32), jnp.zeros((D, D), jnp.float32), jnp.zeros((D, FF), jnp.float32), jnp.zeros((FF,), jnp.float32), jnp.zeros((FF, D), jnp.float32), jnp.zeros((D,), jnp.float32))
    totals, (outputs, gradients) = lax.scan(one_sequence, zero_totals, (regroup(tokens), regroup(cotangent), positions))
    return (ungroup(outputs), ungroup(gradients), totals[0], totals[1], totals[2], totals[3], totals[4], totals[5], totals[6], totals[7], totals[8], totals[9], totals[10])
```

```python
import math

import jax
import jax.numpy as jnp
from jax import lax
from jax.sharding import PartitionSpec as P

HEADS = 12
HEAD_DIM = 64
ROT = 16
EPSILON = 1e-05
HALF = jnp.bfloat16
FULL = jnp.float32


class Grid:
    def __init__(self, axis):
        self.axis = axis
        self.size = lax.axis_size(axis)
        self.inner = 2 if self.size % 2 == 0 else 1
        self.outer = self.size // self.inner
        index = lax.axis_index(axis)
        self.row = index // self.inner
        self.col = index % self.inner

    def owner(self, s, j):
        return ((self.row - s) % self.outer) * self.inner + (self.col - j) % self.inner

    def shift(self, value, rows, cols):
        pairs = []
        for source in range(self.size):
            row = (source // self.inner + rows) % self.outer
            col = (source % self.inner + cols) % self.inner
            pairs.append((source, row * self.inner + col))
        return lax.ppermute(value, self.axis, pairs)

    def slots(self):
        return [(s, j) for s in range(self.outer) for j in range(self.inner)]

    def gather(self, value):
        found = {}
        for s in range(self.outer):
            found[s, 0] = value
            if self.inner == 2:
                found[s, 1] = self.shift(value, 0, 1)
            if s + 1 < self.outer:
                value = self.shift(value, 1, 0)
        return found

    def scatter_sum(self, parts):
        total = None
        for s in reversed(range(self.outer)):
            here = parts[s, 0].astype(FULL)
            if self.inner == 2:
                here = here + self.shift(parts[s, 1].astype(HALF), 0, -1).astype(FULL)
            if total is not None:
                here = here + self.shift(total.astype(HALF), -1, 0).astype(FULL)
            total = here
        return total

    def exchange(self, parts_for):
        found = {}
        for s, j in self.slots():
            target = ((self.row + s) % self.outer) * self.inner + (self.col + j) % self.inner
            piece = parts_for(target)
            found[s, j] = piece if (s, j) == (0, 0) else self.shift(piece, s, j)
        return found

    def place(self, found, axis, dtype):
        first = found[0, 0]
        shape = list(first.shape)
        step = shape[axis]
        shape[axis] = step * self.size
        whole = jnp.zeros(shape, dtype)
        for slot, value in found.items():
            whole = lax.dynamic_update_slice_in_dim(
                whole, value.astype(dtype), self.owner(*slot) * step, axis
            )
        return whole


def normalize(values):
    row_mean = jnp.mean(values, axis=-1, keepdims=True)
    centred = values - row_mean
    variance = jnp.mean(centred * centred, axis=-1, keepdims=True)
    inverse = lax.rsqrt(variance + EPSILON)
    return centred * inverse, inverse


def normalize_back(upstream, normed, inverse, gain):
    scaled = upstream * gain
    first_mean = jnp.mean(scaled, axis=-1, keepdims=True)
    second_mean = jnp.mean(scaled * normed, axis=-1, keepdims=True)
    return inverse * (scaled - first_mean - normed * second_mean)


def block_positions(first_block, count_rows, count_ctx):
    half_rows = count_rows // 2
    offsets = jnp.arange(count_rows, dtype=jnp.int32)
    early_pos = first_block * half_rows + offsets
    late_pos = (2 * count_ctx - 1 - first_block) * half_rows + offsets - half_rows
    return jnp.where(offsets < half_rows, early_pos, late_pos)


def rotary_tables(positions):
    half_rot = ROT // 2
    frequency = jnp.power(10000.0, -2.0 * jnp.arange(half_rot, dtype=FULL) / ROT)
    angles = frequency[:, None] * positions.astype(FULL)[None, :]
    return (jnp.cos(angles), jnp.sin(angles))


def rotate_cols(values, cosine, sine_table):
    half_rot = ROT // 2
    first_half = values[:, :half_rot]
    second = values[:, half_rot:ROT]
    cos_wide = cosine[None]
    sin_wide = sine_table[None]
    return jnp.concatenate(
        [
            first_half * cos_wide - second * sin_wide,
            second * cos_wide + first_half * sin_wide,
            values[:, ROT:],
        ],
        axis=1,
    )


def gelu_parts(values):
    cumulative = 0.5 * (1.0 + lax.erf(values * 0.7071067811865476))
    density = jnp.exp(-0.5 * values * values) * 0.3989422804014327
    return (values * cumulative, cumulative + values * density)


def dot(left, right, left_dim, right_dim):
    return lax.dot_general(
        left, right, (((left_dim,), (right_dim,)), ((), ())), preferred_element_type=FULL
    )


def attend(queries, keys, values, causal, score_scale, head_group):
    mixed_parts = []
    weight_parts = []
    for first in range(0, HEADS, head_group):
        pick = slice(first, first + head_group)
        scores = (
            jnp.einsum("hdq,hdk->hqk", queries[pick], keys[pick], preferred_element_type=FULL)
            * score_scale
        )
        scores = jnp.where(causal[None], scores, -jnp.inf)
        row_peak = jnp.max(scores, axis=-1, keepdims=True)
        weights = jnp.exp(scores - row_peak)
        weights = weights * (1.0 / jnp.sum(weights, axis=-1, keepdims=True))
        weights_half = weights.astype(HALF)
        mixed_parts.append(
            jnp.einsum("hqk,hdk->hdq", weights_half, values[pick], preferred_element_type=FULL)
        )
        weight_parts.append((weights, weights_half))
    return jnp.concatenate(mixed_parts, axis=0), weight_parts


def attend_back(
    queries, keys, values, weight_parts, row_delta, mix_grad, score_scale, head_group
):
    query_parts = []
    key_parts = []
    value_parts = []
    for part, first in enumerate(range(0, HEADS, head_group)):
        pick = slice(first, first + head_group)
        weights, weights_half = weight_parts[part]
        value_parts.append(
            jnp.einsum("hqk,hdq->hdk", weights_half, mix_grad[pick], preferred_element_type=FULL)
        )
        weight_grad = jnp.einsum(
            "hdq,hdk->hqk", mix_grad[pick], values[pick], preferred_element_type=FULL
        )
        score_grad = (
            weights * (weight_grad - row_delta[pick, :, None]) * score_scale
        ).astype(HALF)
        query_parts.append(
            jnp.einsum("hqk,hdk->hdq", score_grad, keys[pick], preferred_element_type=FULL)
        )
        key_parts.append(
            jnp.einsum("hqk,hdq->hdk", score_grad, queries[pick], preferred_element_type=FULL)
        )
    return (
        jnp.concatenate(query_parts, axis=0),
        jnp.concatenate(key_parts, axis=0),
        jnp.concatenate(value_parts, axis=0),
    )


def per_device(
    tokens,
    cotangent,
    pair_order,
    gain_attn,
    shift_attn,
    gain_mlp,
    shift_mlp,
    qkv_weight,
    qkv_bias,
    dense_weight,
    up_weight,
    up_bias,
    down_weight,
    out_bias,
):
    rows, width = tokens.shape
    ctx = Grid("ctx")
    fsdp = Grid("fsdp")
    share = width // fsdp.size
    hidden_share = down_weight.shape[0]
    piece = share // ctx.size
    head_group = math.gcd(HEADS, 4)
    score_scale = 1.0 / math.sqrt(HEAD_DIM)

    small = jnp.concatenate(
        [
            gain_attn[None],
            shift_attn[None],
            gain_mlp[None],
            shift_mlp[None],
            out_bias[None],
            qkv_bias.reshape(3, share),
        ],
        axis=0,
    )
    small_all = fsdp.place(fsdp.gather(small[None]), 0, HALF).astype(FULL)
    feature_rows = jnp.swapaxes(small_all[:, :5], 0, 1).reshape(5, width)
    gainattn_all, shiftattn_all, gainmlp_all, shiftmlp_all, outbias_all = feature_rows
    qkvbias_all = small_all[:, 5:].reshape(3 * width)
    group_tokens = fsdp.gather(tokens)
    group_cot = fsdp.gather(cotangent)
    up_cols = fsdp.place(
        fsdp.exchange(
            lambda device: lax.dynamic_slice_in_dim(up_weight, device * hidden_share, hidden_share, 1)
        ),
        0,
        HALF,
    )
    sequence = ctx.gather(tokens)
    qkv_all = fsdp.place(fsdp.gather(qkv_weight), 0, HALF)
    dense_all = fsdp.place(fsdp.gather(dense_weight), 0, HALF)

    mlp_tokens = jnp.concatenate([group_tokens[slot] for slot in fsdp.slots()], axis=0)
    mlp_cot = jnp.concatenate([group_cot[slot] for slot in fsdp.slots()], axis=0)
    normed_mlp, inverse_mlp = normalize(mlp_tokens.astype(FULL))
    mlp_in = (normed_mlp * gainmlp_all + shiftmlp_all).astype(HALF)
    hidden_pre = dot(mlp_in, up_cols, 1, 0) + up_bias.astype(FULL)
    activated, slope = gelu_parts(hidden_pre)
    hidden = activated.astype(HALF)
    pre_grad = dot(mlp_cot, down_weight, 1, 1) * slope
    upbias_part = jnp.sum(pre_grad, axis=0)
    pre_half = pre_grad.astype(HALF)
    down_part = dot(hidden, mlp_cot, 0, 0)
    up_part = dot(mlp_in, pre_half, 0, 0)
    mlp_out = dot(hidden, down_weight, 1, 0)
    mlp_grad = dot(pre_half, up_cols, 1, 1)
    mlpshift_part = jnp.sum(mlp_grad, axis=0)
    mlpgain_part = jnp.sum(mlp_grad * normed_mlp, axis=0)

    def group_rows(values):
        return {
            slot: values[k * rows : (k + 1) * rows] for k, slot in enumerate(fsdp.slots())
        }

    mlp_own = fsdp.scatter_sum(group_rows(mlp_out))
    mlp_in_grad = fsdp.scatter_sum(group_rows(mlp_grad))

    down_rows = hidden_share // ctx.size
    down_half = down_part.astype(HALF)
    up_half = up_part.astype(HALF).reshape(fsdp.size, ctx.size, piece, hidden_share)
    down_sum = ctx.scatter_sum(
        {
            slot: lax.dynamic_slice_in_dim(down_half, ctx.owner(*slot) * down_rows, down_rows, 0)
            for slot in ctx.slots()
        }
    )
    up_sum = ctx.scatter_sum(
        {
            slot: lax.dynamic_slice_in_dim(up_half, ctx.owner(*slot), 1, 1)[:, 0]
            for slot in ctx.slots()
        }
    )
    down_grad = ctx.place(ctx.gather(down_sum.astype(HALF)), 0, FULL)
    up_sum = up_sum.astype(HALF)
    up_piece = fsdp.place(
        fsdp.exchange(lambda device: lax.dynamic_slice_in_dim(up_sum, device, 1, 0)[0]), 1, HALF
    )
    up_grad = ctx.place(ctx.gather(up_piece), 0, FULL)

    order_row = pair_order[0]
    positions = jnp.concatenate(
        [
            block_positions(order_row[ctx.owner(*slot)], rows, ctx.size) for slot in ctx.slots()
        ]
    )
    causal = positions[None, :] <= positions[:rows, None]
    cosine, sine_table = rotary_tables(positions)
    own_cos, own_sin = cosine[:, :rows], sine_table[:, :rows]
    attn_tokens = jnp.concatenate([sequence[slot] for slot in ctx.slots()], axis=0)
    normed_attn, inverse_attn = normalize(attn_tokens.astype(FULL))
    attn_in = (normed_attn * gainattn_all + shiftattn_all).astype(HALF)
    length = attn_in.shape[0]
    pairs_cols = dot(qkv_all[:, width:], attn_in, 0, 1) + qkvbias_all[width:, None]
    query_cols = dot(qkv_all[:, :width], attn_in[:rows], 0, 1) + qkvbias_all[:width, None]
    queries = rotate_cols(
        query_cols.reshape(HEADS, HEAD_DIM, rows), own_cos, own_sin
    ).astype(HALF)
    keys = rotate_cols(
        pairs_cols[:width].reshape(HEADS, HEAD_DIM, length), cosine, sine_table
    ).astype(HALF)
    values = pairs_cols[width:].reshape(HEADS, HEAD_DIM, length).astype(HALF)
    mixed, weight_parts = attend(queries, keys, values, causal, score_scale, head_group)
    attn_mix = mixed.astype(HALF)
    mix_cols = attn_mix.reshape(width, rows)
    residual = tokens.astype(FULL)
    layer_out = (residual + dot(mix_cols, dense_all, 0, 0) + mlp_own + outbias_all).astype(HALF)

    grad_out = cotangent.astype(FULL)
    outbias_part = jnp.sum(grad_out, axis=0)
    dense_part = dot(mix_cols, cotangent, 1, 0)
    mix_grad = dot(dense_all, cotangent, 1, 1).astype(HALF).reshape(HEADS, HEAD_DIM, rows)
    row_delta = jnp.sum(mix_grad.astype(FULL) * attn_mix.astype(FULL), axis=1)
    query_grad, key_grad, value_grad = attend_back(
        queries, keys, values, weight_parts, row_delta, mix_grad, score_scale, head_group
    )
    query_grad = rotate_cols(query_grad, own_cos, -own_sin).reshape(width, rows)
    key_grad = rotate_cols(key_grad, cosine, -sine_table).reshape(width, length)
    pair_grad = jnp.concatenate([key_grad, value_grad.reshape(width, length)], axis=0)
    qkvbias_part = jnp.concatenate([jnp.sum(query_grad, axis=1), jnp.sum(pair_grad, axis=1)])
    query_half = query_grad.astype(HALF)
    pair_half = pair_grad.astype(HALF)
    query_part = dot(attn_in[:rows], query_half, 0, 1)
    pair_part = dot(attn_in, pair_half, 0, 1)
    attn_grad = dot(pair_half, qkv_all[:, width:], 0, 1)
    attn_grad = attn_grad.at[:rows].add(dot(query_half, qkv_all[:, :width], 0, 1))
    attnshift_part = jnp.sum(attn_grad, axis=0)
    attngain_part = jnp.sum(attn_grad * normed_attn, axis=0)
    attn_in_grad = ctx.scatter_sum(
        {slot: attn_grad[k * rows : (k + 1) * rows] for k, slot in enumerate(ctx.slots())}
    )
    into_attn = normalize_back(
        attn_in_grad, normed_attn[:rows], inverse_attn[:rows], gainattn_all
    )
    into_mlp = normalize_back(mlp_in_grad, normed_mlp[:rows], inverse_mlp[:rows], gainmlp_all)
    input_grad = grad_out + into_attn + into_mlp

    own = jnp.arange(fsdp.size) == fsdp.row * fsdp.inner + fsdp.col
    upbias_wide = jnp.where(own[:, None], upbias_part[None], 0.0)
    strip = jnp.concatenate(
        [
            attngain_part.reshape(fsdp.size, share),
            attnshift_part.reshape(fsdp.size, share),
            mlpgain_part.reshape(fsdp.size, share),
            mlpshift_part.reshape(fsdp.size, share),
            outbias_part.reshape(fsdp.size, share),
            qkvbias_part.reshape(fsdp.size, 3 * share),
            upbias_wide,
        ],
        axis=1,
    )
    per_piece = strip.shape[1] // ctx.size
    lanes = -(-per_piece // (piece * 128)) * 128
    strip = strip.reshape(fsdp.size * ctx.size, per_piece)
    strip = jnp.pad(strip, ((0, 0), (0, piece * lanes - per_piece))).reshape(width, lanes)
    joined = jnp.concatenate(
        [
            query_part.astype(HALF),
            pair_part.astype(HALF),
            dense_part.astype(HALF),
            strip.astype(HALF),
        ],
        axis=1,
    )
    joined = fsdp.scatter_sum(
        {
            slot: lax.dynamic_slice_in_dim(joined, fsdp.owner(*slot) * share, share, 0)
            for slot in fsdp.slots()
        }
    )
    joined = joined.astype(HALF)
    joined = ctx.scatter_sum(
        {
            slot: lax.dynamic_slice_in_dim(joined, ctx.owner(*slot) * piece, piece, 0)
            for slot in ctx.slots()
        }
    )
    joined = ctx.place(ctx.gather(joined.astype(HALF)), 0, FULL)
    qkv_grad = joined[:, : 3 * width]
    dense_grad = joined[:, 3 * width : 4 * width]
    strip = joined[:, 4 * width :].reshape(ctx.size, piece * lanes)[:, :per_piece].reshape(-1)
    return (
        layer_out,
        input_grad,
        strip[:share],
        strip[share : 2 * share],
        strip[2 * share : 3 * share],
        strip[3 * share : 4 * share],
        qkv_grad,
        strip[5 * share : 8 * share],
        dense_grad,
        up_grad,
        strip[8 * share :],
        down_grad,
        strip[4 * share : 5 * share],
    )


def solution(mesh):
    return jax.shard_map(
        per_device,
        mesh=mesh,
        in_specs=(
            P(("ctx", "fsdp"), None),
            P(("ctx", "fsdp"), None),
            P("fsdp", None),
            P("fsdp"),
            P("fsdp"),
            P("fsdp"),
            P("fsdp"),
            P("fsdp", None),
            P("fsdp"),
            P("fsdp", None),
            P("fsdp", None),
            P("fsdp"),
            P("fsdp", None),
            P("fsdp"),
        ),
        out_specs=(
            P(("ctx", "fsdp"), None),
            P(("ctx", "fsdp"), None),
            P("fsdp"),
            P("fsdp"),
            P("fsdp"),
            P("fsdp"),
            P("fsdp", None),
            P("fsdp"),
            P("fsdp", None),
            P("fsdp", None),
            P("fsdp"),
            P("fsdp", None),
            P("fsdp"),
        ),
        check_vma=False,
    )
```

```python
import math

import jax
import jax.numpy as jnp
from jax import lax
from jax.experimental import pallas as pl
from jax.experimental.pallas import tpu as pltpu
from jax.sharding import PartitionSpec as P


HEAD_DIM = 64
ROT = 16
EPSILON = 1e-05
HALF = jnp.bfloat16
FULL = jnp.float32


class Grid:
    def __init__(self, axis):
        self.axis = axis
        self.seen = {}
        self.size = lax.axis_size(axis)
        self.inner = 2 if self.size % 2 == 0 else 1
        self.outer = self.size // self.inner
        index = lax.axis_index(axis)
        self.row = index // self.inner
        self.col = index % self.inner

    def back(self, s, j):
        return (self.row - s) % self.outer, (self.col - j) % self.inner

    def shift(self, value, rows, cols, name="mv"):
        pairs = []
        for source in range(self.size):
            row = (source // self.inner + rows) % self.outer
            col = (source % self.inner + cols) % self.inner
            pairs.append((source, row * self.inner + col))
        self.seen[name] = lax.ppermute(value, self.axis, pairs)
        return self.seen[name]

    def slots(self):
        return [(s, j) for j in range(self.inner) for s in range(self.outer)]

    def gather(self, value, name="mv"):
        found = {}
        for s in range(self.outer):
            found[s, 0] = value
            if self.inner == 2:
                found[s, 1] = self.shift(value, 0, 1, f"{name}n{s}")
            if s + 1 < self.outer:
                value = self.shift(value, 1, 0, f"{name}f{s}")
        return found

    def slot_sum(self, keep, send, name="mv"):
        parts = self.slot_terms(keep, send, name)
        return sum((part.astype(FULL) for part in parts[1:]), start=parts[0])

    def slot_terms(self, keep, send, name):
        parts = [keep[s].astype(FULL) for s in range(self.outer)]
        if self.inner == 2:
            there = self.shift(send.astype(HALF), 0, -1, name + "n")
            parts = [part + there[s].astype(FULL) for s, part in enumerate(parts)]
        return parts[:1] + [
            self.shift(parts[s].astype(HALF), -s, 0, f"{name}f{s}") for s in range(1, self.outer)
        ]

    def halves(self, stack):
        return stack[: self.outer], stack[self.outer :]

    def chunk(self, s, j):
        row, col = self.back(s, j)
        return col * self.outer + row

    def chunk_sum(self, arrays, name="mv"):
        parts = self.chunk_parts(arrays, name)
        return sum((part.astype(FULL) for part in parts[1:]), start=parts[0])

    def chunk_parts(self, arrays, name):
        steps = [whole.shape[1] // self.size for whole in arrays]

        def cut(wholes, starts, sizes):
            return [
                lax.dynamic_slice_in_dim(whole, start, size, 1)
                for whole, start, size in zip(wholes, starts, sizes)
            ]

        halves = [step * self.outer for step in steps]
        mine = cut(arrays, [self.col * half for half in halves], halves)
        if self.inner == 2:
            other = cut(arrays, [(1 - self.col) * half for half in halves], halves)
            there = self.shift(jnp.concatenate(other, axis=0).astype(HALF), 0, 1, name + "n")
        parts = []
        for s in range(self.outer):
            row = (self.row - s) % self.outer
            part = jnp.concatenate(cut(mine, [row * step for step in steps], steps), axis=0)
            part = part.astype(FULL)
            if self.inner == 2:
                got = lax.dynamic_slice_in_dim(there, row * steps[0], steps[0], 1)
                part = part + got.astype(FULL)
            parts.append(self.shift(part.astype(HALF), -s, 0, f"{name}f{s}") if s else part)
        return parts

    def exchange(self, value, axis, name="mv"):
        step = value.shape[axis] // self.size
        wide = step * self.inner
        found = {}
        sent = []
        for s in range(self.outer):
            row = (self.row + s) % self.outer
            piece = lax.dynamic_slice_in_dim(value, row * wide, wide, axis)
            piece = piece if s == 0 else self.shift(piece, s, 0, f"{name}f{s}")
            found[s, 0] = lax.dynamic_slice_in_dim(piece, self.col * step, step, axis)
            if self.inner == 2:
                sent.append(lax.dynamic_slice_in_dim(piece, (1 - self.col) * step, step, axis))
        if self.inner == 2:
            there = self.shift(jnp.stack(sent), 0, 1, name + "n")
            for s in range(self.outer):
                found[s, 1] = there[s]
        return found

    def gather_late(self, value, name="mv"):
        rows = [value]
        rows += [self.shift(value, s, 0, f"{name}f{s}") for s in range(1, self.outer)]
        there = None
        if self.inner == 2:
            there = self.shift(jnp.stack(rows), 0, 1, name + "n")
        return rows, there

    def reorder(self, value, axis, ordered):
        step = value.shape[axis] // self.size
        if (self.inner, self.outer) == (2, 2):
            blocks = [lax.slice_in_dim(value, k * step, (k + 1) * step, axis=axis) for k in range(4)]
            a, b, c, d = (blocks[0], blocks[2], blocks[1], blocks[3])
            if not ordered:
                a, b, c, d = blocks
            flip_col = self.col == 1
            a, b, c, d = (
                jnp.where(flip_col, b, a),
                jnp.where(flip_col, a, b),
                jnp.where(flip_col, d, c),
                jnp.where(flip_col, c, d),
            )
            flip_row = self.row == 1
            a, b, c, d = (
                jnp.where(flip_row, c, a),
                jnp.where(flip_row, d, b),
                jnp.where(flip_row, a, c),
                jnp.where(flip_row, b, d),
            )
            picked = [a, b, c, d] if ordered else [a, c, b, d]
            return jnp.concatenate(picked, axis=axis)
        starts = []
        if ordered:
            for row in range(self.outer):
                for col in range(self.inner):
                    s, j = (self.row - row) % self.outer, (self.col - col) % self.inner
                    starts.append(j * self.outer + s)
        else:
            for s, j in self.slots():
                row, col = self.back(s, j)
                starts.append(row * self.inner + col)
        return jnp.concatenate(
            [lax.dynamic_slice_in_dim(value, k * step, step, axis) for k in starts], axis=axis
        )

    def line_up(self, found, axis=0):
        return jnp.concatenate([found[slot] for slot in self.slots()], axis=axis)


def after(value, *first):
    return lax.optimization_barrier((value, *first))[0]


def unpack(found):
    rows, there = found
    places = [(k, None) for k in range(len(rows))]
    if there is None:
        return rows, places
    return [*rows, there], places + [(len(rows), k) for k in range(len(rows))]


def chunk_starts(grid, step):
    return jnp.stack([grid.chunk(*slot) * step for slot in grid.slots()])


def place_rows(founds, grid, outputs, turn_last=False):
    step = founds[0][0][0].shape[0]
    starts = chunk_starts(grid, step)
    widths = [sum(cut[3] for cut in cuts) for cuts in outputs]
    shapes = [jax.ShapeDtypeStruct((step * grid.size, wide), FULL) for wide in widths]
    last = outputs[-1][0][3] if turn_last else 0
    arrays = []
    sets = []
    for found in founds:
        found_arrays, places = unpack(found)
        sets.append([(len(arrays) + k, lead) for k, lead in places])
        arrays += found_arrays

    def pick(refs, which, k):
        number, lead = sets[which][k]
        return refs[number] if lead is None else refs[number].at[lead]

    if step % 8:
        results = []
        for cuts, shape in zip(outputs, shapes):
            whole = jnp.zeros(shape.shape, FULL)
            for which, source, target, wide in cuts:
                for k in range(grid.size):
                    number, lead = sets[which][k]
                    value = arrays[number] if lead is None else arrays[number][lead]
                    value = value[:, source : source + wide].astype(FULL)
                    whole = lax.dynamic_update_slice(whole, value, (starts[k], target))
            results.append(whole)
        return results + [results[-1].T] if turn_last else results

    def kernel(starts_ref, *refs):
        outs = refs[len(arrays) :]
        for k in range(grid.size):
            rows = pl.ds(pl.multiple_of(starts_ref[k], 8), step)
            for out, cuts in zip(outs, outputs):
                for which, source, target, wide in cuts:
                    value = pick(refs, which, k)[:, source : source + wide]
                    out[rows, target : target + wide] = value.astype(FULL)
        if turn_last:
            outs[-1][...] = outs[-2][...].T

    if turn_last:
        shapes.append(jax.ShapeDtypeStruct((last, step * grid.size), FULL))
    return pl.pallas_call(
        kernel,
        out_shape=shapes,
        in_specs=[pl.BlockSpec(memory_space=pltpu.SMEM)]
        + [pl.BlockSpec(memory_space=pltpu.VMEM)] * len(arrays),
        out_specs=[pl.BlockSpec(memory_space=pltpu.VMEM)] * len(shapes),
        name="pr",
    )(starts, *arrays)


def place_blocks(found, grid, groups, columns):
    arrays, places = unpack(found)
    _, step, width = arrays[0].shape
    block = step * grid.size
    starts = chunk_starts(grid, step)
    if step % 8 or width % 128:
        low = jnp.zeros((groups, block, width), FULL)
        high = jnp.zeros((block, groups * width), FULL)
        for k, (number, lead) in enumerate(places):
            value = (arrays[number] if lead is None else arrays[number][lead]).astype(FULL)
            low = lax.dynamic_update_slice_in_dim(low, value[:groups], starts[k], 1)
            for g in range(groups):
                high = lax.dynamic_update_slice(
                    high, value[groups + g], (starts[k], columns[g] * width)
                )
        return low.reshape(groups * block, width), high

    def kernel(starts_ref, columns_ref, *refs):
        low, high = refs[len(arrays) :]
        for k, (number, lead) in enumerate(places):
            ref = refs[number] if lead is None else refs[number].at[lead]
            start = starts_ref[k]
            for g in range(groups):
                low[pl.ds(pl.multiple_of(g * block + start, 8), step), :] = ref[g].astype(FULL)
                lanes = pl.ds(pl.multiple_of(columns_ref[g] * width, 128), width)
                high[pl.ds(pl.multiple_of(start, 8), step), lanes] = ref[groups + g].astype(FULL)

    return pl.pallas_call(
        kernel,
        out_shape=[
            jax.ShapeDtypeStruct((groups * block, width), FULL),
            jax.ShapeDtypeStruct((block, groups * width), FULL),
        ],
        in_specs=[pl.BlockSpec(memory_space=pltpu.SMEM)] * 2
        + [pl.BlockSpec(memory_space=pltpu.VMEM)] * len(arrays),
        out_specs=[pl.BlockSpec(memory_space=pltpu.VMEM)] * 2,
        name="pb",
    )(starts, jnp.stack(columns), *arrays)


def stack_columns(parts, cuts):
    step = parts[0].shape[0]

    def kernel(*refs):
        for out, (first, last) in zip(refs[len(parts) :], cuts):
            for k in range(len(parts)):
                out[k * step : (k + 1) * step, :] = refs[k][:, first:last]

    return pl.pallas_call(
        kernel,
        out_shape=[
            jax.ShapeDtypeStruct((step * len(parts), last - first), parts[0].dtype)
            for first, last in cuts
        ],
        in_specs=[pl.BlockSpec(memory_space=pltpu.VMEM)] * len(parts),
        out_specs=[pl.BlockSpec(memory_space=pltpu.VMEM)] * len(cuts),
        name="sc",
    )(*parts)


def slot_places(grid):
    places = []
    for row in range(grid.outer):
        for col in range(grid.inner):
            s, j = (grid.row - row) % grid.outer, (grid.col - col) % grid.inner
            places.append(j * grid.outer + s)
    return jnp.stack(places)


def small_rows(parts, grid, share):
    width = share * grid.size
    places = slot_places(grid)

    def kernel(places_ref, *refs):
        rows = [ref[...].astype(FULL) for ref in refs[: len(parts)]]
        out, bias = refs[len(parts) :]
        for k in range(2):
            line = [row[:, k * share : (k + 1) * share] for row in rows]
            out[k : k + 1, :] = jnp.concatenate(line, axis=1)
        ordered = []
        for g in range(grid.size):
            picked = rows[0]
            for k in range(1, grid.size):
                picked = jnp.where(places_ref[g] == k, rows[k], picked)
            ordered.append(picked)
        for k in range(2, 5):
            line = [row[:, k * share : (k + 1) * share] for row in ordered]
            out[k : k + 1, :] = jnp.concatenate(line, axis=1)
        out[5:6, :] = jnp.concatenate([row[:, :share] for row in ordered], axis=1)
        bias[...] = jnp.concatenate([row[:, 5 * share :] for row in ordered], axis=1)

    return pl.pallas_call(
        kernel,
        out_shape=[
            jax.ShapeDtypeStruct((8, width), FULL),
            jax.ShapeDtypeStruct((1, 3 * width), FULL),
        ],
        in_specs=[pl.BlockSpec(memory_space=pltpu.SMEM)]
        + [pl.BlockSpec(memory_space=pltpu.VMEM)] * len(parts),
        out_specs=[pl.BlockSpec(memory_space=pltpu.VMEM)] * 2,
        name="smr",
    )(places, *parts)


def normalize(values):
    row_mean = jnp.mean(values, axis=-1, keepdims=True)
    centred = values - row_mean
    variance = jnp.mean(centred * centred, axis=-1, keepdims=True)
    inverse = lax.rsqrt(variance + EPSILON)
    return centred * inverse, inverse


def normalize_back(upstream, normed, inverse, gain):
    scaled = upstream * gain
    first_mean = jnp.mean(scaled, axis=-1, keepdims=True)
    second_mean = jnp.mean(scaled * normed, axis=-1, keepdims=True)
    return inverse * (scaled - first_mean - normed * second_mean)


def slot_positions(order_row, grid, rows):
    half_rows = rows // 2
    number = jnp.arange(grid.size, dtype=jnp.int32)
    row = (grid.row - number % grid.outer) % grid.outer
    col = (grid.col - number // grid.outer) % grid.inner
    chosen = (row * grid.inner + col)[:, None] == number[None, :]
    first_block = jnp.sum(jnp.where(chosen, order_row[None, :], 0), axis=1)[:, None]
    offsets = jnp.arange(rows, dtype=jnp.int32)[None, :]
    early_pos = first_block * half_rows + offsets
    late_pos = (2 * grid.size - 1 - first_block) * half_rows + offsets - half_rows
    return jnp.where(offsets < half_rows, early_pos, late_pos).reshape(-1)


def rotary_tables(positions):
    half_rot = ROT // 2
    frequency = jnp.power(10000.0, -2.0 * jnp.arange(half_rot, dtype=FULL) / ROT)
    angles = frequency[:, None] * positions.astype(FULL)[None, :]
    return (jnp.cos(angles), jnp.sin(angles))


def gelu_parts(values):
    cumulative = 0.5 * (1.0 + lax.erf(values * 0.7071067811865476))
    density = jnp.exp(-0.5 * values * values) * 0.3989422804014327
    return (values * cumulative, cumulative + values * density)


def dot(left, right, left_dim, right_dim):
    return lax.dot_general(
        left, right, (((left_dim,), (right_dim,)), ((), ())), preferred_element_type=FULL
    )


def sequence_norm(parts, features):
    width = parts[0].shape[-1]
    pieces = []
    for k, part in enumerate(parts):
        pieces += [(k, None)] if part.ndim == 2 else [(k, lead) for lead in range(part.shape[0])]
    rows = parts[0].shape[0]
    length = rows * len(pieces)

    def kernel(*refs):
        feature_ref, in_ref, turned_ref, own_ref, normed_ref = refs[len(parts) :]
        for block, (k, lead) in enumerate(pieces):
            value = refs[k][...] if lead is None else refs[k][lead]
            normed, _ = normalize(value.astype(FULL))
            scaled = normed * feature_ref[0:1, :] + feature_ref[1:2, :]
            span = slice(block * rows, (block + 1) * rows)
            normed_ref[span, :] = normed
            in_ref[span, :] = scaled.astype(HALF)
            turned = scaled.T.astype(HALF)
            turned_ref[:, span] = turned
            if block == 0:
                own_ref[...] = turned

    return pl.pallas_call(
        kernel,
        out_shape=[
            jax.ShapeDtypeStruct((length, width), HALF),
            jax.ShapeDtypeStruct((width, length), HALF),
            jax.ShapeDtypeStruct((width, rows), HALF),
            jax.ShapeDtypeStruct((length, width), FULL),
        ],
        in_specs=[pl.BlockSpec(memory_space=pltpu.VMEM)] * (len(parts) + 1),
        out_specs=[pl.BlockSpec(memory_space=pltpu.VMEM)] * 4,
        name="sn",
    )(*parts, features)


def weight_grads(terms, grid, step):
    count = len(terms)
    wides = [right.shape[-1 if dim == 0 else -2] for _, right, dim, _ in terms]
    wide = sum(wides)

    def kernel(*refs):
        keep, send = refs[2 * count :]
        first = 0
        for term, (_, _, dim, lead) in enumerate(terms):
            right = refs[2 * term + 1][...] if lead is None else refs[2 * term + 1][lead]
            product = dot(refs[2 * term][...], right, 1, dim).astype(HALF)
            last = first + wides[term]
            for k in range(grid.size):
                out = keep if k < grid.outer else send
                out[k % grid.outer, :, first:last] = product[k * step : (k + 1) * step]
            first = last

    flops = sum(2 * left.size * size for (left, _, _, _), size in zip(terms, wides))
    return pl.pallas_call(
        kernel,
        out_shape=[
            jax.ShapeDtypeStruct((grid.outer, step, wide), HALF),
            jax.ShapeDtypeStruct((grid.outer * (grid.inner - 1), step, wide), HALF),
        ],
        in_specs=[pl.BlockSpec(memory_space=pltpu.VMEM)] * (2 * count),
        out_specs=[pl.BlockSpec(memory_space=pltpu.VMEM)] * 2,
        cost_estimate=pl.CostEstimate(
            flops=flops, bytes_accessed=4 * wide * step * grid.size, transcendentals=0
        ),
        name="wg",
    )(*(value for left, right, _, _ in terms for value in (left, right)))


def token_grads(terms, mlp_grad, tokens, cotangent, features, grid):
    rows, width = tokens.shape
    share = width // grid.size

    def kernel(places_ref, *refs):
        mlp_ref, token_ref, cot_ref, feature_ref, out_ref = refs[len(terms) :]
        total = refs[0][...].astype(FULL)
        for ref in refs[1 : len(terms)]:
            total = total + ref[...].astype(FULL)
        blocks = []
        for g in range(grid.size):
            picked = total[:, :share]
            for k in range(1, grid.size):
                picked = jnp.where(places_ref[g] == k, total[:, k * share : (k + 1) * share], picked)
            blocks.append(picked)
        normed, inverse = normalize(token_ref[...].astype(FULL))
        result = cot_ref[...].astype(FULL)
        result += normalize_back(
            jnp.concatenate(blocks, axis=1), normed, inverse, feature_ref[5:6, :]
        )
        out_ref[...] = result + normalize_back(mlp_ref[...], normed, inverse, feature_ref[2:3, :])

    return pl.pallas_call(
        kernel,
        out_shape=jax.ShapeDtypeStruct((rows, width), FULL),
        in_specs=[pl.BlockSpec(memory_space=pltpu.SMEM)]
        + [pl.BlockSpec(memory_space=pltpu.VMEM)] * (len(terms) + 4),
        out_specs=pl.BlockSpec(memory_space=pltpu.VMEM),
        name="tg",
    )(slot_places(grid), *terms, mlp_grad, tokens, cotangent, features)


def turn(values, cosine, sine_table):
    half_rot = ROT // 2
    first_half = values[:half_rot]
    second = values[half_rot:ROT]
    return jnp.concatenate(
        [
            first_half * cosine - second * sine_table,
            second * cosine + first_half * sine_table,
            values[ROT:],
        ],
        axis=0,
    )


def attention(query_cols, pair_cols, bias, mix_grad, positions, cosine, sine_table):
    width, rows = query_cols.shape
    length = pair_cols.shape[1]
    per_step = 2
    lanes = per_step * HEAD_DIM
    score_scale = 1.0 / math.sqrt(HEAD_DIM)

    def kernel(q_ref, k_ref, v_ref, qb_ref, kb_ref, vb_ref, g_ref, pos_ref, cos_ref, sin_ref, mix_ref, turned_ref, dq_ref, pair_ref, sum_ref):
        cosine, sine_table = cos_ref[...], sin_ref[...]
        own_cos, own_sin = cosine[:, :rows], sine_table[:, :rows]
        spread = jnp.broadcast_to(pos_ref[:, :rows], (8, rows)).T[:, :1]
        causal = pos_ref[...] <= spread
        biases = jnp.concatenate([qb_ref[...], kb_ref[...], vb_ref[...]] + [jnp.zeros((5, lanes), FULL)], axis=0).T
        mixes = []
        for head in range(per_step):
            dims = slice(head * HEAD_DIM, (head + 1) * HEAD_DIM)
            query = turn(q_ref[dims, :] + biases[dims, 0:1], own_cos, own_sin)
            query = query * score_scale
            query_rows = query.T.astype(HALF)
            query = query.astype(HALF)
            key = turn(k_ref[dims, :] + biases[dims, 1:2], cosine, sine_table).astype(HALF)
            value = (v_ref[dims, :] + biases[dims, 2:3]).astype(HALF)
            grad = g_ref[:, dims]
            scores = jnp.dot(query_rows, key, preferred_element_type=FULL)
            scores = jnp.where(causal, scores, -jnp.inf)
            weights = jnp.exp(scores - jnp.max(scores, axis=1, keepdims=True))
            weights = weights * (1.0 / jnp.sum(weights, axis=1, keepdims=True))
            weights_half = weights.astype(HALF)
            mix = dot(weights_half, value, 1, 1)
            turned_ref[dims, :] = mix.T.astype(HALF)
            mix = mix.astype(HALF)
            mixes.append(mix)
            delta = jnp.sum(grad.astype(FULL) * mix.astype(FULL), axis=1, keepdims=True)
            weight_grad = jnp.dot(grad, value, preferred_element_type=FULL)
            score_grad = (weights * (weight_grad - delta)).astype(HALF)
            value_grad = jnp.dot(grad.astype(FULL).T.astype(HALF), weights_half, preferred_element_type=FULL)
            key_grad = turn(jnp.dot(query, score_grad, preferred_element_type=FULL), cosine, -sine_table)
            query_grad = turn(dot(key, score_grad, 1, 1) * score_scale, own_cos, -own_sin)
            dq_ref[dims, :] = query_grad.astype(HALF)
            pair_ref[0, dims, :] = key_grad.astype(HALF)
            pair_ref[1, dims, :] = value_grad.astype(HALF)
            for k, part in enumerate((query_grad, key_grad, value_grad)):
                sum_ref[dims, k : k + 1] = jnp.sum(part, axis=1, keepdims=True)
        mix_ref[...] = jnp.concatenate(mixes, axis=1)

    flops = width // HEAD_DIM * 2 * rows * length * HEAD_DIM * 6
    return pl.pallas_call(
        kernel,
        grid=(width // lanes,),
        out_shape=[
            jax.ShapeDtypeStruct((rows, width), HALF),
            jax.ShapeDtypeStruct((width, rows), HALF),
            jax.ShapeDtypeStruct((width, rows), HALF),
            jax.ShapeDtypeStruct((2, width, length), HALF),
            jax.ShapeDtypeStruct((width, 8), FULL),
        ],
        in_specs=[
            pl.BlockSpec((lanes, rows), lambda i: (i, 0)),
            pl.BlockSpec((lanes, length), lambda i: (i, 0)),
            pl.BlockSpec((lanes, length), lambda i: (i + width // lanes, 0)),
            pl.BlockSpec((1, lanes), lambda i: (0, i)),
            pl.BlockSpec((1, lanes), lambda i: (0, i + width // lanes)),
            pl.BlockSpec((1, lanes), lambda i: (0, i + 2 * (width // lanes))),
            pl.BlockSpec((rows, lanes), lambda i: (0, i)),
            pl.BlockSpec((1, length), lambda i: (0, 0)),
            pl.BlockSpec((ROT // 2, length), lambda i: (0, 0)),
            pl.BlockSpec((ROT // 2, length), lambda i: (0, 0)),
        ],
        out_specs=[
            pl.BlockSpec((rows, lanes), lambda i: (0, i)),
            pl.BlockSpec((lanes, rows), lambda i: (i, 0)),
            pl.BlockSpec((lanes, rows), lambda i: (i, 0)),
            pl.BlockSpec((2, lanes, length), lambda i: (0, i, 0)),
            pl.BlockSpec((lanes, 8), lambda i: (i, 0)),
        ],
        cost_estimate=pl.CostEstimate(
            flops=flops * 4, bytes_accessed=14 * width * length, transcendentals=width // HEAD_DIM * rows * length
        ),
        name="at",
    )(
        query_cols,
        pair_cols,
        pair_cols,
        bias,
        bias,
        bias,
        mix_grad,
        positions[None, :].astype(FULL),
        cosine,
        sine_table,
    )


def strip_rows(placed, in_order, bias_sums, grid, share):
    count = len(placed) + len(in_order)
    width = share * grid.size
    owners = []
    for slot in grid.slots():
        row, col = grid.back(*slot)
        owners.append(row * grid.inner + col)

    def kernel(owners_ref, *refs):
        out = refs[-1]
        sums = refs[count][...].T
        ordered = []
        for g in range(grid.size):
            rows = [ref[:, g * share : (g + 1) * share] for ref in refs[len(placed) : count]]
            for k in range(3):
                which, first = divmod((3 * g + k) * share, width)
                rows.append(sums[which : which + 1, first : first + share])
            ordered.append(jnp.concatenate(rows, axis=0))
        for k in range(grid.size):
            for row, ref in enumerate(refs[: len(placed)]):
                out[k, row : row + 1, :] = ref[:, k * share : (k + 1) * share]
            picked = ordered[0]
            for g in range(1, grid.size):
                picked = jnp.where(owners_ref[k] == g, ordered[g], picked)
            out[k, len(placed) :, :] = picked

    return pl.pallas_call(
        kernel,
        out_shape=jax.ShapeDtypeStruct((grid.size, count + 3, share), FULL),
        in_specs=[pl.BlockSpec(memory_space=pltpu.SMEM)]
        + [pl.BlockSpec(memory_space=pltpu.VMEM)] * (count + 1),
        out_specs=pl.BlockSpec(memory_space=pltpu.VMEM),
        name="sr",
    )(jnp.stack(owners), *(row[None] for row in (*placed, *in_order)), bias_sums)


def per_device(
    tokens,
    cotangent,
    pair_order,
    gain_attn,
    shift_attn,
    gain_mlp,
    shift_mlp,
    qkv_weight,
    qkv_bias,
    dense_weight,
    up_weight,
    up_bias,
    down_weight,
    out_bias,
):
    rows, width = tokens.shape
    ctx = Grid("ctx")
    fsdp = Grid("fsdp")
    groups = fsdp.size
    share = width // groups
    hidden_share = down_weight.shape[0]

    group_tokens = fsdp.gather(tokens, "gt")
    group_cot = fsdp.gather(cotangent, "gc")
    up_cols = fsdp.exchange(up_weight, 1, "up")
    sequence, others = ctx.gather_late(fsdp.reorder(tokens, 1, False), "tk")
    if others is not None:
        sequence = [*sequence, others]
    early = (*group_tokens.values(), *group_cot.values())
    small = jnp.concatenate(
        [
            gain_attn,
            shift_attn,
            gain_mlp,
            shift_mlp,
            out_bias,
            qkv_bias,
        ]
    )
    small = fsdp.gather(small.reshape(1, 8 * share), "sm")
    features, qkvbias_all = small_rows([small[slot] for slot in fsdp.slots()], fsdp, share)
    _, _, gainmlp_all, shiftmlp_all, outbias_all = (
        features[k : k + 1] for k in range(5)
    )
    qkv_slots = fsdp.gather(after(qkv_weight, fsdp.seen.get("upf1", tokens)), "qk")
    up_cols = {slot: after(piece, *early) for slot, piece in up_cols.items()}
    dense_slots = fsdp.line_up(
        fsdp.gather(after(dense_weight, qkv_slots[fsdp.outer - 1, 0]), "dn")
    )

    up_cols = fsdp.reorder(fsdp.line_up(up_cols), 0, True)

    mlp_tokens = fsdp.line_up(group_tokens)
    mlp_cot = fsdp.line_up(group_cot)
    normed_mlp, _ = normalize(mlp_tokens.astype(FULL))
    mlp_in = (normed_mlp * gainmlp_all + shiftmlp_all).astype(HALF)
    hidden_pre = dot(mlp_in, up_cols, 1, 0)
    hidden_pre = hidden_pre + up_bias.astype(FULL)
    activated, slope = gelu_parts(hidden_pre)
    hidden = activated.astype(HALF)
    pre_grad = dot(mlp_cot, down_weight, 1, 1) * slope
    upbias_part = jnp.sum(pre_grad, axis=0)
    pre_half = pre_grad.astype(HALF)
    down_part = dot(hidden, mlp_cot, 0, 0).astype(HALF)
    up_part = dot(mlp_in, pre_half, 0, 0).astype(HALF).reshape(groups, share, hidden_share)
    late = after(down_weight, down_part, up_part)
    mlp_out = dot(hidden, late, 1, 0)
    mlp_grad = dot(pre_half, after(up_cols, late), 1, 1)
    mlpshift_part = jnp.sum(mlp_grad, axis=0)
    mlpgain_part = jnp.sum(mlp_grad * normed_mlp, axis=0)

    joint = hidden_share == width
    if joint:
        down_part = down_part.reshape(groups, share, width)
        mlp_parts = ctx.chunk_parts([down_part, up_part], "ml")

    both = jnp.concatenate([mlp_out, mlp_grad], axis=1).astype(HALF)
    both = fsdp.slot_sum(*fsdp.halves(both.reshape(groups, rows, 2 * width)), "bo")
    mlp_own, mlp_in_grad = both[:, :width], both[:, width:]

    positions = slot_positions(pair_order[0], ctx, rows)
    cosine, sine_table = rotary_tables(positions)
    attn_in, attn_turned, own_turned, normed_attn = sequence_norm(sequence, features)
    query_weight, pair_weight = stack_columns(
        [qkv_slots[slot] for slot in fsdp.slots()], [(0, width), (width, 3 * width)]
    )
    query_cols = dot(query_weight, attn_in[:rows], 0, 1)
    pair_cols = dot(pair_weight, attn_in, 0, 1)
    dense_all = fsdp.reorder(dense_slots, 0, True)
    mix_grad = dot(cotangent, dense_all, 1, 1).astype(HALF)
    mix, mix_turned, query_grad, pair_grad, bias_sums = attention(
        query_cols, pair_cols, qkvbias_all, mix_grad, positions, cosine, sine_table
    )
    if joint:
        mlp_sum = mlp_parts[0]
        for part in mlp_parts[1:]:
            mlp_sum = mlp_sum + after(part, mix).astype(FULL)
        mlp_sum = mlp_sum.astype(HALF)
        up_piece = fsdp.line_up(fsdp.exchange(mlp_sum[groups:], 0, "ug"))
        mlp_sum = jnp.concatenate([mlp_sum[:groups], up_piece], axis=0)
        columns = []
        for slot in fsdp.slots():
            row, col = fsdp.back(*slot)
            columns.append(row * fsdp.inner + col)
        mlp_found = ctx.gather_late(mlp_sum, "ma")
        down_grad, up_grad = place_blocks(mlp_found, ctx, groups, columns)
    else:
        down_sum = ctx.chunk_sum([down_part[None]]).astype(HALF)[0]
        (down_grad,) = place_rows((ctx.gather_late(down_sum),), ctx, [[(0, 0, 0, width)]])
        up_piece = fsdp.exchange(ctx.chunk_sum([up_part]).astype(HALF), 0)
        up_piece = fsdp.reorder(fsdp.line_up(up_piece, 2), 2, True)[0]
        (up_grad,) = place_rows((ctx.gather_late(up_piece),), ctx, [[(0, 0, 0, up_weight.shape[1])]])

    first_keep, first_send = weight_grads(
        ((own_turned, query_grad, 1, None), (attn_turned, pair_grad, 1, 0)), fsdp, share
    )
    value_grad = after(pair_grad, first_send)
    mix_turned = fsdp.reorder(mix_turned, 0, False)
    second_keep, second_send = weight_grads(
        ((attn_turned, value_grad, 1, 1), (mix_turned, cotangent, 0, None)), fsdp, share
    )
    first_terms = fsdp.slot_terms(first_keep, first_send, "ga")
    first_sum = sum((term.astype(FULL) for term in first_terms[1:]), start=first_terms[0])
    first_sum = first_sum.astype(HALF)
    second_sum = fsdp.slot_sum(second_keep, second_send, "gb")
    pair_grad = after(pair_grad.reshape(2 * width, -1), second_send)
    attn_grad = dot(pair_grad, pair_weight, 0, 1)
    own_grad = attn_grad[:rows] + dot(query_grad, query_weight, 0, 1)
    attn_grad = jnp.concatenate([own_grad, attn_grad[rows:]], axis=0)
    attnshift_part = jnp.sum(attn_grad, axis=0)
    attngain_part = jnp.sum(attn_grad * normed_attn, axis=0)
    input_terms = ctx.slot_terms(*ctx.halves(attn_grad.astype(HALF).reshape(ctx.size, rows, width)), "in")

    residual = tokens.astype(FULL)
    outbias_part = jnp.sum(cotangent.astype(FULL), axis=0)
    layer_out = (residual + dot(mix, dense_all, 1, 0) + mlp_own + outbias_all).astype(HALF)
    input_grad = token_grads(input_terms, mlp_in_grad, tokens, cotangent, features, fsdp)

    strip = strip_rows(
        (attngain_part, attnshift_part),
        (mlpgain_part, mlpshift_part, outbias_part),
        bias_sums,
        fsdp,
        share,
    )
    strip = fsdp.slot_sum(*fsdp.halves(strip), "st")
    strip = jnp.concatenate([strip, upbias_part.reshape(-1, share)], axis=0)
    strip = jnp.pad(strip, ((0, 128 - strip.shape[0]), (0, 0))).T.astype(HALF)
    second_sum = jnp.concatenate([second_sum.astype(HALF), strip], axis=1)
    founds = []
    for name, total in (("ga", first_sum), ("gb", second_sum)):
        total = ctx.chunk_sum([total[None]], name + "c")[0]
        founds.append(ctx.gather_late(total.astype(HALF), name + "a"))
    qkv_grad, dense_grad, _, strip = place_rows(
        founds,
        ctx,
        [
            [(0, 0, 0, 2 * width), (1, 0, 2 * width, width)],
            [(1, width, 0, width)],
            [(1, 2 * width, 0, 128)],
        ],
        turn_last=True,
    )
    return (
        layer_out,
        input_grad,
        strip[0],
        strip[1],
        strip[2],
        strip[3],
        qkv_grad,
        strip[5:8].reshape(-1),
        dense_grad,
        up_grad,
        strip[8 : 8 + hidden_share // share].reshape(-1),
        down_grad,
        strip[4],
    )


def solution(mesh):
    return jax.shard_map(
        per_device,
        mesh=mesh,
        in_specs=(
            P(("ctx", "fsdp"), None),
            P(("ctx", "fsdp"), None),
            P("fsdp", None),
            P("fsdp"),
            P("fsdp"),
            P("fsdp"),
            P("fsdp"),
            P("fsdp", None),
            P("fsdp"),
            P("fsdp", None),
            P("fsdp", None),
            P("fsdp"),
            P("fsdp", None),
            P("fsdp"),
        ),
        out_specs=(
            P(("ctx", "fsdp"), None),
            P(("ctx", "fsdp"), None),
            P("fsdp"),
            P("fsdp"),
            P("fsdp"),
            P("fsdp"),
            P("fsdp", None),
            P("fsdp"),
            P("fsdp", None),
            P("fsdp", None),
            P("fsdp"),
            P("fsdp", None),
            P("fsdp"),
        ),
        check_vma=False,
    )
```
